32 devices in a mesh: mem: 2 (over x), gy: 4 (over z), gx: 4 (over y, core).
Axes of the slice: x: 2, y: 2, z: 4, core: 2. Of those that a mesh axis runs over, the one named last changes fastest.
Arguments:
- alpha: float32 [16, 32, 64, 512], P('mem', None, 'gy', 'gx'), may hold values from -4 to 4
- perturb: bfloat16 [16, 4, 32, 64, 512], P('mem', None, None, 'gy', 'gx'), may hold values from -6 to 6
- chi: float32 [4, 32, 64, 512], P(None, None, 'gy', 'gx'), may hold values from -4 to 4
- kappa: float32 [64, 512], P('gy', 'gx'), may hold values from 0.05 to 0.24
- vert_bounds: int32 [2, 32], replicated, may hold values from 0 to 31, as said below
- static_vert: float32 [4, 32, 32], replicated, may hold values from -1 to 1
- fine_owner: int32 [16, 2], P(('gy', 'gx')), may hold values from 0 to 1, each once within a row
- obs_stencil: int32 [32768], P(('mem', 'gy', 'gx')), may hold values from 0 to 959
- obs_weight: float32 [4, 32768], P(None, ('mem', 'gy', 'gx')), may hold values from 0.05 to 0.5
- background: bfloat16 [32768, 128], P(('mem', 'gy', 'gx')), may hold values from -6 to 6
- observed: float32 [8, 32768], P(None, ('mem', 'gy', 'gx')), may hold values from -6 to 6
- inv_var: float32 [8, 32768], P(None, ('mem', 'gy', 'gx')), may hold values from 2 to 32
- jacobian: float32 [8, 128], replicated, may hold values from -0.5 to 0.5
- obs_count: int32 [32], P(('mem', 'gy', 'gx')), may hold values from 256 to 1024, as said below
Outputs:
- grad_alpha: float32 [16, 32, 64, 512], P('mem', None, 'gy', 'gx')
- grad_chi: float32 [4, 32, 64, 512], P(None, None, 'gy', 'gx')
The draws below stay inside these ranges and needn't reach their ends.
Inputs may be any that keep to these rules, and one draw needn't show every extreme that they name: `vert_bounds`: row 0 holds each level's lowest and row 1 its highest coupled level; level l lies between both inclusive, and each lies 1 to 4 levels from l unless cut at the ends of the column. `obs_count`: observations below this count in a device's block are live; some device has exactly 1024 and some exactly 256.
All inputs are finite; a program needn't handle non-finite values.
Results may differ from the reference program's by a relative error of at most 0.00099.
Values may be sent and summed in bfloat16 or wider, within the bound.
A program may use at most 128 MiB of HBM per device.

```python
import math
import jax
import jax.numpy as jnp
from jax import lax

MEMBERS = 16
L = 32
V = 4
VL = 128
TY = 16
TX = 128
NY = 64
NX = 512
TILES = 16
FB = 64
SHIFT = 32
NDIFF = 4
VREACH = 4
OBS_DEV = 1024
OBS_TOTAL = 32768
NCHAN = 8
N_MEM = 2
N_GX = 4
DEVICES = 32


def draw_vert_bounds(key, part):
    key_low, key_high = jax.random.split(jax.random.fold_in(key, 11))
    level = jnp.arange(L, dtype=jnp.int32)
    lower = jnp.maximum(level - jax.random.randint(key_low, (L,), 1, VREACH + 1), 0)
    upper = jnp.minimum(level + jax.random.randint(key_high, (L,), 1, VREACH + 1), L - 1)
    return jnp.stack([lower, upper]).astype(jnp.int32)


def draw_obs_count(key, part):
    key_count, key_pick = jax.random.split(jax.random.fold_in(key, 23))
    counts = jax.random.randint(key_count, (DEVICES,), OBS_DEV // 4, OBS_DEV + 1)
    order = jax.random.permutation(key_pick, DEVICES)
    counts = counts.at[order[0]].set(OBS_DEV).at[order[1]].set(OBS_DEV // 4)
    return counts.astype(jnp.int32)


def plant(result, stream_key, least, largest):
    longest = result.shape.index(max(result.shape))
    spots = []
    for shift in (0, 1):
        where = [jax.random.randint(jax.random.fold_in(stream_key, axis), (), 0, length) for axis, length in enumerate(result.shape)]
        where[longest] = (where[longest] + shift) % result.shape[longest]
        spots.append(tuple(where))
    return result.at[spots[0]].set(least).at[spots[1]].set(largest)


def level_of(own_key, extent, pieces, low, top_value):
    def one(dim, parts):
        draws = jax.random.uniform(jax.random.fold_in(jax.random.fold_in(own_key, 6), dim), (parts,), jnp.float32, low / len(pieces), top_value / len(pieces))
        return jnp.repeat(jnp.exp(draws), extent[dim] // parts).reshape((-1,) + (1,) * (len(extent) - dim - 1))

    gain = one(*pieces[0])
    for cut in pieces[1:]:
        gain = gain * one(*cut)
    return gain


def normal_values(rng, extent, width, limit, cuts=(), kind=jnp.bfloat16):
    result = width * jax.random.normal(rng, extent, jnp.float32)
    if cuts:
        result = result * level_of(rng, extent, cuts, -0.22, 0.18)
    return jnp.clip(result, -limit, limit).astype(kind)


def setup_inputs(seed: int = 0) -> dict:
    key_of = jax.random.split(jax.random.key(seed), 15)
    return {
        "alpha": normal_values(key_of[0], (MEMBERS, L, NY, NX), 0.5, 4.0, ((0, 2), (2, 4), (3, 4)), jnp.float32),
        "perturb": normal_values(key_of[1], (MEMBERS, V, L, NY, NX), 1.0, 6.0, ((0, 2), (3, 4), (4, 4))),
        "chi": normal_values(key_of[2], (V, L, NY, NX), 0.5, 4.0, ((2, 4), (3, 4)), jnp.float32),
        "kappa": jnp.clip(jnp.exp(math.log(0.24) - 1.5686159 * jax.random.uniform(key_of[3], (NY, NX), jnp.float32) ** level_of(key_of[3], (NY, NX), ((0, 4), (1, 4)), -0.2, 0.2)), 0.05, 0.24),
        "vert_bounds": draw_vert_bounds(jax.random.fold_in(key_of[14], 71), 0),
        "static_vert": normal_values(key_of[5], (V, L, L), L ** -0.5, 1.0, (), jnp.float32),
        "fine_owner": jax.vmap(lambda own: jax.random.permutation(own, N_MEM))(jax.random.split(key_of[6], TILES)).reshape((TILES, N_MEM)).astype(jnp.int32),
        "obs_stencil": plant(jax.random.randint(key_of[7], (OBS_TOTAL,), 0, (TY - 1) * FB), jax.random.fold_in(key_of[7], 1), 0, ((TY - 1) * FB) - 1).astype(jnp.int32),
        "obs_weight": jnp.clip(0.05 + 0.45 * jax.random.uniform(key_of[8], (4, OBS_TOTAL), jnp.float32) ** level_of(key_of[8], (4, OBS_TOTAL), ((1, 32),), -0.2, 0.2), 0.05, 0.5),
        "background": normal_values(key_of[9], (OBS_TOTAL, VL), 1.0, 6.0, ((0, 32),)),
        "observed": normal_values(key_of[10], (NCHAN, OBS_TOTAL), 1.0, 6.0, ((1, 32),), jnp.float32),
        "inv_var": jnp.clip(jnp.exp(math.log(32.0) - 2.7725887 * jax.random.uniform(key_of[11], (NCHAN, OBS_TOTAL), jnp.float32) ** level_of(key_of[11], (NCHAN, OBS_TOTAL), ((1, 32),), -0.2, 0.2)), 2.0, 32.0),
        "jacobian": normal_values(key_of[12], (NCHAN, VL), VL ** -0.5, 0.5, (), jnp.float32),
        "obs_count": draw_obs_count(jax.random.fold_in(key_of[14], 71), 0),
    }


ensemble_weight = 0.8
static_weight = 0.6
vertical_scale = 2.0
highest = lax.Precision.HIGHEST

def vertical_matrix(vert_bounds, levels):
    row_level = lax.broadcasted_iota(jnp.int32, (levels, levels), 0)
    col_level = lax.broadcasted_iota(jnp.int32, (levels, levels), 1)
    inside = (col_level >= vert_bounds[0][:, None]) & (col_level <= vert_bounds[1][:, None])
    distance = jnp.abs(row_level - col_level).astype(jnp.float32)
    return jnp.where(inside, jnp.exp(-distance / vertical_scale), jnp.zeros_like(distance))

def laplace(values):
    from_north = jnp.concatenate([values[:, :, :1], values[:, :, :-1]], axis=2)
    from_south = jnp.concatenate([values[:, :, 1:], values[:, :, -1:]], axis=2)
    return from_north + from_south + jnp.roll(values, 1, axis=3) + jnp.roll(values, -1, axis=3) - 4.0 * values

def reference(alpha, perturb, chi, kappa, vert_bounds, static_vert, fine_owner, obs_stencil, obs_weight, background, observed, inv_var, jacobian, obs_count):
    column_width = V * L
    ens_scale = ensemble_weight / math.sqrt(MEMBERS - 1)
    vertical = vertical_matrix(vert_bounds, L)
    spread = jnp.einsum('lm,kmyx->klyx', vertical, alpha, precision=highest)
    for repeat in range(NDIFF):
        spread = spread + kappa * laplace(spread)

    def add_member(carry, paired):
        member_pert, member_spread = paired
        return (carry + member_pert.astype(jnp.float32) * member_spread[None], 0)
    member_total, unused = lax.scan(add_member, jnp.zeros((V, L, NY, NX), jnp.float32), (perturb, spread))
    static = jnp.einsum('vlm,vmyx->vlyx', static_vert, chi, precision=highest)
    increment = (ens_scale * member_total + static_weight * static).astype(jnp.bfloat16)
    flat_increment = increment.reshape(column_width, NY * NX)
    obs_index = jnp.arange(OBS_TOTAL, dtype=jnp.int32)
    obs_device = (obs_index // OBS_DEV).astype(jnp.int32)
    member_group = (obs_device // TILES).astype(jnp.int32)
    tile_index = (obs_device % TILES).astype(jnp.int32)
    owners = fine_owner[tile_index]
    band_ids = lax.broadcasted_iota(jnp.int32, owners.shape, 1)
    band_index = lax.optimization_barrier(jnp.sum(jnp.where(owners == member_group[:, None], band_ids, jnp.zeros_like(band_ids)), axis=1)).astype(jnp.int32)
    anchor_row = (obs_stencil // FB).astype(jnp.int32)
    anchor_col = (obs_stencil % FB).astype(jnp.int32)
    base_row = tile_index // N_GX * TY + anchor_row
    base_col = tile_index % N_GX * TX + band_index * FB + SHIFT + anchor_col
    cells_of = jnp.stack([((base_row + corner // 2) * NX + (base_col + corner % 2) % NX).astype(jnp.int32) for corner in range(4)])
    increment_obs = jnp.zeros((OBS_TOTAL, column_width), jnp.float32)
    for corner in range(4):
        picked = jnp.take(flat_increment, cells_of[corner], axis=1).T.astype(jnp.float32)
        increment_obs = increment_obs + obs_weight[corner][:, None] * picked
    bent = jnp.tanh(background.astype(jnp.float32) + increment_obs)
    modeled = jnp.einsum('cv,ov->co', jacobian, bent, precision=highest)
    live = obs_index % OBS_DEV < obs_count[obs_device]
    misfit = jnp.where(live[None, :], (modeled - observed) * inv_var, jnp.zeros_like(modeled))
    state_grad = (1.0 - bent * bent) * jnp.einsum('co,cv->ov', misfit, jacobian, precision=highest)
    global_grad = jnp.zeros((column_width, NY * NX), jnp.float32)
    for corner in range(4):
        global_grad = global_grad.at[:, cells_of[corner]].add((obs_weight[corner][:, None] * state_grad).T)
    gradient = global_grad.reshape(V, L, NY, NX)
    grad_chi = chi + static_weight * jnp.einsum('vlm,vlyx->vmyx', static_vert, gradient, precision=highest)

    def member_back(member_pert):
        return ens_scale * lax.optimization_barrier(jnp.sum(member_pert.astype(jnp.float32) * gradient, axis=0))
    back_spread = lax.map(member_back, perturb)
    for repeat in range(NDIFF):
        back_spread = back_spread + laplace(kappa * back_spread)
    grad_alpha = alpha + jnp.einsum('lm,klyx->kmyx', vertical, back_spread, precision=highest)
    return (grad_alpha, grad_chi)
```

```python
import math

import jax
import jax.numpy as jnp
from jax import lax
from jax.experimental import pallas as pl
from jax.experimental.pallas import tpu as pltpu
from jax.sharding import PartitionSpec as P

NDIFF = 4

ensemble_weight = 0.8
static_weight = 0.6
vertical_scale = 2.0
highest = lax.Precision.HIGHEST
f32 = jnp.float32
bf16 = jnp.bfloat16
NT = (((1,), (1,)), ((), ()))
TN = (((0,), (0,)), ((), ()))


def shifted(value, axis, steps):
    count = lax.axis_size(axis)
    pairs = [(source, (source + steps) % count) for source in range(count)]
    return lax.ppermute(value, axis, pairs)


def vertical_matrix(vert_bounds, levels):
    row_level = lax.broadcasted_iota(jnp.int32, (levels, levels), 0)
    col_level = lax.broadcasted_iota(jnp.int32, (levels, levels), 1)
    inside = (col_level >= vert_bounds[0][:, None]) & (col_level <= vert_bounds[1][:, None])
    distance = jnp.abs(row_level - col_level).astype(f32)
    return jnp.where(inside, jnp.exp(-distance / vertical_scale), jnp.zeros_like(distance))


def edge_picker(width, depth):
    row = lax.broadcasted_iota(jnp.int32, (2 * depth, width), 0)
    col = lax.broadcasted_iota(jnp.int32, (2 * depth, width), 1)
    return jnp.where(col == jnp.where(row < depth, row, width - 2 * depth + row), 1.0, 0.0)


def params(grid_dims=0):
    if grid_dims:
        return pltpu.CompilerParams(
            dimension_semantics=("arbitrary",) * grid_dims, vmem_limit_bytes=56 << 20
        )
    return pltpu.CompilerParams(vmem_limit_bytes=56 << 20)


def write_edges(tile, rows_ref, cols_ref, rows, depth):
    width = tile(0).shape[1]
    for d in range(depth):
        rows_ref[0, 0, d] = tile(d).astype(bf16)
        rows_ref[1, 0, d] = tile(rows - depth + d).astype(bf16)
    picker = edge_picker(width, depth).astype(bf16)
    stack = jnp.concatenate([tile(y).astype(bf16) for y in range(rows)], axis=0)
    picked = lax.dot_general(picker, stack, NT, preferred_element_type=f32)
    cols_ref[0, 0] = picked[:depth].astype(bf16)
    cols_ref[1, 0] = picked[depth:].astype(bf16)


def pack_kernel(rows, levels, depth, field_ref, rows_ref, cols_ref):
    write_edges(
        lambda y: field_ref[0, pl.ds(y, levels, stride=rows), :], rows_ref, cols_ref, rows, depth
    )


def edge_shapes(members, rows, levels, width, depth):
    shapes = [
        jax.ShapeDtypeStruct((2, members, depth, levels, width), bf16),
        jax.ShapeDtypeStruct((2, members, depth, rows * levels), bf16),
    ]
    specs = [
        pl.BlockSpec((2, 1, depth, levels, width), lambda k: (0, k, 0, 0, 0)),
        pl.BlockSpec((2, 1, depth, rows * levels), lambda k: (0, k, 0, 0)),
    ]
    return shapes, specs


def exchange(row_edges, col_edges, rows, levels, depth):
    gy = lax.axis_size("gy")
    up = [(i, i - 1) for i in range(1, gy)]
    down = [(i, i + 1) for i in range(gy - 1)]
    from_east = shifted(col_edges[0], "gx", -1)
    from_west = shifted(col_edges[1], "gx", 1)
    south = lax.ppermute(row_edges[0], "gy", up)
    north = lax.ppermute(row_edges[1], "gy", down)
    sides = jnp.concatenate([from_east, from_west], axis=1)
    part = depth * levels
    corner_south = lax.ppermute(sides[:, :, :part], "gy", up)
    corner_north = lax.ppermute(sides[:, :, -part:], "gy", down)
    ring = jnp.concatenate([sides, corner_south, corner_north], axis=2)
    return south, north, ring


def kappa_ring(kappa, depth):
    rows, width = kappa.shape
    gy = lax.axis_size("gy")
    turned = kappa.T
    east = shifted(turned[:depth], "gx", -1).T
    west = shifted(turned[-depth:], "gx", 1).T
    wide = jnp.concatenate([kappa, east, jnp.zeros((rows, width - 2 * depth), f32), west], axis=1)
    south = lax.ppermute(wide[:depth], "gy", [(i, i - 1) for i in range(1, gy)])
    north = lax.ppermute(wide[-depth:], "gy", [(i, i + 1) for i in range(gy - 1)])
    return jnp.concatenate([wide, south, north], axis=0)


def fill_ring(tile, south_ref, north_ref, sides_ref, ring, rows, levels, width, depth):
    total = rows + 2 * depth
    for y in range(rows):
        ring[y, :, :width] = tile(y)
    for d in range(depth):
        ring[rows + d, :, :width] = south_ref[0, d].astype(f32)
        ring[rows + depth + d, :, :width] = north_ref[0, d].astype(f32)
    picker = edge_picker(width, depth).astype(bf16)
    side = lax.dot_general(sides_ref[0], picker, TN, preferred_element_type=f32)
    for y in range(total):
        ring[y, :, width:] = side[y * levels : (y + 1) * levels]


def diffuse(ring_a, ring_b, kappa_ref, edge_ref, rows, width, depth, adjoint):
    total = rows + 2 * depth
    at_top = edge_ref[0] == 1
    at_bottom = edge_ref[1] == 1
    source, target = ring_a, ring_b
    for step in range(1, depth + 1):
        wanted = list(range(rows + depth - step)) + list(range(rows + depth + step, total))
        keep = width if step == depth else 2 * width

        def load(y):
            value = source[y]
            return kappa_ref[pl.ds(y, 1), :] * value if adjoint else value

        for y in wanted:
            center = load(y)
            north = load((y - 1) % total)
            south = load((y + 1) % total)
            if y == 0:
                north = jnp.where(at_top, center, north)
            if y == rows - 1:
                south = jnp.where(at_bottom, center, south)
            west = pltpu.roll(center, 1, 1)
            east = pltpu.roll(center, 2 * width - 1, 1)
            change = ((north + south) + (west + east)) - 4.0 * center
            if adjoint:
                result = source[y] + change
            else:
                result = center + kappa_ref[pl.ds(y, 1), :] * change
            target[y, :, :keep] = result[:, :keep]
        source, target = target, source
    return source


def forward_kernel(
    dims, ens_scale, edge_ref, alpha_ref, south_ref, north_ref, sides_ref, kappa_ref, vertical_ref,
    perturb_ref, static_ref, out_ref, ring_a, ring_b, spread, acc,
):
    rows, levels, width, variables, depth = dims
    step = pl.program_id(0)
    fill_ring(
        lambda y: alpha_ref[0, pl.ds(y, levels, stride=rows), :],
        south_ref, north_ref, sides_ref, ring_a, rows, levels, width, depth,
    )
    done = diffuse(ring_a, ring_b, kappa_ref, edge_ref, rows, width, depth, False)
    for y in range(rows):
        spread[pl.ds(y, levels, stride=rows), :] = jnp.dot(
            vertical_ref[...], done[y, :, :width], precision=highest, preferred_element_type=f32
        )

    @pl.when(step == 0)
    def _():
        acc[...] = jnp.zeros_like(acc)

    count = rows * levels
    for v in range(variables):
        acc[v * count : (v + 1) * count] += perturb_ref[0, v].astype(f32) * spread[...]

    @pl.when(step == pl.num_programs(0) - 1)
    def _():
        for y in range(rows):
            column = acc[pl.ds(y, variables * levels, stride=rows), :]
            out_ref[y] = ens_scale * column.T + static_ref[y]


def backward_kernel(
    dims, ens_scale, perturb_ref, grad_ref, main_ref, rows_ref, cols_ref, grad, field,
):
    rows, levels, width, variables, depth = dims

    @pl.when(pl.program_id(0) == 0)
    def _():
        for y in range(rows):
            grad[pl.ds(y, variables * levels, stride=rows), :] = ens_scale * grad_ref[y].T

    count = rows * levels
    total = perturb_ref[0, 0].astype(f32) * grad[:count]
    for v in range(1, variables):
        total = total + perturb_ref[0, v].astype(f32) * grad[v * count : (v + 1) * count]
    field[...] = total
    for y in range(rows):
        main_ref[0, y] = field[pl.ds(y, levels, stride=rows), :]
    write_edges(
        lambda y: field[pl.ds(y, levels, stride=rows), :], rows_ref, cols_ref, rows, depth
    )


def adjoint_kernel(
    dims, edge_ref, alpha_ref, main_ref, south_ref, north_ref, sides_ref, kappa_ref, vertical_ref,
    out_ref, ring_a, ring_b,
):
    rows, levels, width, variables, depth = dims
    fill_ring(
        lambda y: main_ref[0, y],
        south_ref, north_ref, sides_ref, ring_a, rows, levels, width, depth,
    )
    done = diffuse(ring_a, ring_b, kappa_ref, edge_ref, rows, width, depth, True)
    for y in range(rows):
        out_ref[0, pl.ds(y, levels, stride=rows), :] = alpha_ref[
            0, pl.ds(y, levels, stride=rows), :
        ] + jnp.dot(
            vertical_ref[...], done[y, :, :width], precision=highest, preferred_element_type=f32
        )


def split(value):
    high = value.astype(bf16)
    return high, (value - high.astype(f32)).astype(bf16)


def observe_kernel(
    rows, band, padded, count_ref, table_ref, anchor_ref, weight_ref, background_ref, observed_ref,
    inv_var_ref, jacobian_ref, out_ref, high_ref, low_ref,
):
    places = anchor_ref.shape[1]
    anchor = anchor_ref[...]
    anchor_row = anchor // band
    anchor_col = anchor - anchor_row * band
    slot = lax.broadcasted_iota(jnp.int32, (padded, places), 0)
    at_left = slot == anchor_col
    at_right = slot == anchor_col + 1
    total = background_ref[...].astype(f32).T
    for y in range(rows):
        upper = anchor_row == y
        lower = anchor_row == y - 1
        zero = jnp.zeros(anchor.shape, f32)
        left = jnp.where(upper, weight_ref[0:1], jnp.where(lower, weight_ref[2:3], zero))
        right = jnp.where(upper, weight_ref[1:2], jnp.where(lower, weight_ref[3:4], zero))
        weights = jnp.where(at_left, left, jnp.where(at_right, right, 0.0))
        high, low = split(weights)
        high_ref[y] = high
        low_ref[y] = low
        cells = table_ref[y]
        total = total + lax.dot_general(cells, high, TN, preferred_element_type=f32)
        total = total + lax.dot_general(cells, low, TN, preferred_element_type=f32)
    bent = jnp.tanh(total)
    modeled = jnp.dot(jacobian_ref[...], bent, precision=highest, preferred_element_type=f32)
    position = lax.broadcasted_iota(jnp.int32, modeled.shape, 1)
    misfit = jnp.where(
        position < count_ref[0], (modeled - observed_ref[...]) * inv_var_ref[...], 0.0
    )
    back = lax.dot_general(
        jacobian_ref[...], misfit, TN, precision=highest, preferred_element_type=f32
    )
    state_high, state_low = split((1.0 - bent * bent) * back)
    for y in range(rows):
        high = high_ref[y]
        cells = lax.dot_general(high, state_high, NT, preferred_element_type=f32)
        cells = cells + lax.dot_general(low_ref[y], state_high, NT, preferred_element_type=f32)
        cells = cells + lax.dot_general(high, state_low, NT, preferred_element_type=f32)
        out_ref[y] = cells


def choose(index, options):
    result = options[0]
    for place in range(1, len(options)):
        result = jnp.where(index == place, options[place], result)
    return result


def body(
    alpha, perturb, chi, kappa, vert_bounds, static_vert, fine_owner, obs_stencil, obs_weight,
    background, observed, inv_var, jacobian, obs_count,
):
    members, levels, rows, width = alpha.shape
    variables = perturb.shape[1]
    column = variables * levels
    depth = NDIFF
    groups = lax.axis_size("mem")
    band = width // groups
    shift = band // 2
    rim = shift + 1
    me = lax.axis_index("mem")
    count = rows * levels
    places = obs_stencil.shape[0]
    dims = (rows, levels, width, variables, depth)
    ens_scale = ensemble_weight / math.sqrt(members * groups - 1)
    gy_place = lax.axis_index("gy")
    edge = jnp.stack([gy_place == 0, gy_place == lax.axis_size("gy") - 1]).astype(jnp.int32)
    owners = fine_owner[0]
    band_ids = lax.iota(jnp.int32, groups)

    def band_of(group):
        return jnp.sum(jnp.where(owners == group, band_ids, 0))

    smem = pl.BlockSpec(memory_space=pltpu.SMEM)
    vmem = pl.BlockSpec(memory_space=pltpu.VMEM)
    member_block = pl.BlockSpec((1, count, width), lambda k: (k, 0, 0))
    row_block = pl.BlockSpec((1, depth, levels, width), lambda k: (k, 0, 0, 0))
    side_block = pl.BlockSpec((1, 2 * depth, (rows + 2 * depth) * levels), lambda k: (k, 0, 0))
    perturb_block = pl.BlockSpec((1, variables, count, width), lambda k: (k, 0, 0, 0))
    ring_scratch = pltpu.VMEM((rows + 2 * depth, levels, 2 * width), f32)
    edge_out, edge_specs = edge_shapes(members, rows, levels, width, depth)

    alpha_flat = alpha.reshape(members, count, width)
    perturb_flat = perturb.reshape(members, variables, count, width)
    vertical = vertical_matrix(vert_bounds, levels)

    row_edges, col_edges = pl.pallas_call(
        lambda *refs: pack_kernel(rows, levels, depth, *refs),
        grid=(members,),
        in_specs=[member_block],
        out_specs=edge_specs,
        out_shape=edge_out,
        compiler_params=params(1),
        name="pack",
    )(alpha_flat)
    south, north, sides = exchange(row_edges, col_edges, rows, levels, depth)
    kappa_all = kappa_ring(kappa, depth)

    static = jnp.einsum("vlm,vmyx->yxvl", static_vert, chi, precision=highest)
    static = jnp.where(me == 0, static_weight * static, 0.0).reshape(rows, width, column)
    partial = pl.pallas_call(
        lambda *refs: forward_kernel(dims, ens_scale, *refs),
        grid=(members,),
        in_specs=[
            smem, member_block, row_block, row_block, side_block, vmem, vmem, perturb_block, vmem,
        ],
        out_specs=pl.BlockSpec((rows, width, column), lambda k: (0, 0, 0)),
        out_shape=jax.ShapeDtypeStruct((rows, width, column), f32),
        scratch_shapes=[
            ring_scratch,
            ring_scratch,
            pltpu.VMEM((count, width), f32),
            pltpu.VMEM((variables * count, width), f32),
        ],
        compiler_params=params(1),
        name="forward",
    )(edge, alpha_flat, south, north, sides, kappa_all, vertical, perturb_flat, static)

    east_rim = shifted(partial[:, :rim].astype(bf16), "gx", -1)
    wide = jnp.concatenate([partial, east_rim.astype(f32)], axis=1)
    regions = [wide[:, b * band + shift : b * band + shift + band + 1] for b in range(groups)]
    own_band = band_of(me)
    increment = choose(own_band, regions)
    for hop in range(1, groups):
        away = choose(band_of((me + hop) % groups), regions).astype(bf16)
        increment = increment + shifted(away, "mem", hop).astype(f32)
    padded = -(-(band + 1) // 16) * 16
    table = jnp.pad(increment.astype(bf16), ((0, 0), (0, padded - band - 1), (0, 0)))

    region_grad = pl.pallas_call(
        lambda *refs: observe_kernel(rows, band, padded, *refs),
        in_specs=[smem] + [vmem] * 7,
        out_specs=vmem,
        out_shape=jax.ShapeDtypeStruct((rows, padded, column), f32),
        scratch_shapes=[
            pltpu.VMEM((rows, padded, places), bf16),
            pltpu.VMEM((rows, padded, places), bf16),
        ],
        compiler_params=params(),
        name="observe",
    )(
        obs_count, table, obs_stencil.reshape(1, places), obs_weight, background, observed,
        inv_var, jacobian,
    )

    region_grad = region_grad[:, : band + 1]
    pieces = [(own_band, region_grad)]
    for hop in range(1, groups):
        pieces.append((band_of((me - hop) % groups), shifted(region_grad, "mem", hop)))
    wide_grad = jnp.zeros((rows, width + rim, column), f32)
    for b in range(groups):
        placed = choose_equal(b, pieces)
        before = b * band + shift
        after = width + rim - before - band - 1
        wide_grad = wide_grad + jnp.pad(placed, ((0, 0), (before, after), (0, 0)))
    west_rim = shifted(wide_grad[:, width:], "gx", 1)
    grad_cells = wide_grad[:, :width] + jnp.pad(west_rim, ((0, 0), (0, width - rim), (0, 0)))

    main, row_edges, col_edges = pl.pallas_call(
        lambda *refs: backward_kernel(dims, ens_scale, *refs),
        grid=(members,),
        in_specs=[perturb_block, vmem],
        out_specs=[pl.BlockSpec((1, rows, levels, width), lambda k: (k, 0, 0, 0))] + edge_specs,
        out_shape=[jax.ShapeDtypeStruct((members, rows, levels, width), f32)] + edge_out,
        scratch_shapes=[
            pltpu.VMEM((variables * count, width), f32),
            pltpu.VMEM((count, width), f32),
        ],
        compiler_params=params(1),
        name="backward",
    )(perturb_flat, grad_cells)
    south, north, sides = exchange(row_edges, col_edges, rows, levels, depth)
    grad_chi = chi + static_weight * jnp.einsum(
        "vlm,yxvl->vmyx",
        static_vert,
        grad_cells.reshape(rows, width, variables, levels),
        precision=highest,
    )
    grad_alpha = pl.pallas_call(
        lambda *refs: adjoint_kernel(dims, *refs),
        grid=(members,),
        in_specs=[
            smem, member_block, pl.BlockSpec((1, rows, levels, width), lambda k: (k, 0, 0, 0)),
            row_block, row_block, side_block, vmem, vmem,
        ],
        out_specs=member_block,
        out_shape=jax.ShapeDtypeStruct((members, count, width), f32),
        scratch_shapes=[ring_scratch, ring_scratch],
        compiler_params=params(1),
        name="adjoint",
    )(edge, alpha_flat, main, south, north, sides, kappa_all, vertical.T)
    return (grad_alpha.reshape(alpha.shape), grad_chi)


def choose_equal(wanted, pieces):
    result = pieces[0][1]
    for index, piece in pieces[1:]:
        result = jnp.where(index == wanted, piece, result)
    return result


def solution(mesh):
    in_specs = (
        P("mem", None, "gy", "gx"),
        P("mem", None, None, "gy", "gx"),
        P(None, None, "gy", "gx"),
        P("gy", "gx"),
        P(),
        P(),
        P(("gy", "gx"), None),
        P(("mem", "gy", "gx")),
        P(None, ("mem", "gy", "gx")),
        P(("mem", "gy", "gx"), None),
        P(None, ("mem", "gy", "gx")),
        P(None, ("mem", "gy", "gx")),
        P(),
        P(("mem", "gy", "gx")),
    )
    out_specs = (P("mem", None, "gy", "gx"), P(None, None, "gy", "gx"))
    return jax.shard_map(body, mesh=mesh, in_specs=in_specs, out_specs=out_specs, check_vma=False)
```

```python
import math

import jax
import jax.numpy as jnp
from jax import lax
from jax.experimental import pallas as pl
from jax.experimental.pallas import tpu as pltpu
from jax.sharding import PartitionSpec as P

NDIFF = 4

ensemble_weight = 0.8
static_weight = 0.6
vertical_scale = 2.0
highest = lax.Precision.HIGHEST
f32 = jnp.float32
bf16 = jnp.bfloat16
NT = (((1,), (1,)), ((), ()))
TN = (((0,), (0,)), ((), ()))


def shifted(value, axis, steps):
    count = lax.axis_size(axis)
    pairs = [(source, (source + steps) % count) for source in range(count)]
    return lax.ppermute(value, axis, pairs)


def vertical_matrix(vert_bounds, levels):
    row_level = lax.broadcasted_iota(jnp.int32, (levels, levels), 0)
    col_level = lax.broadcasted_iota(jnp.int32, (levels, levels), 1)
    inside = (col_level >= vert_bounds[0][:, None]) & (col_level <= vert_bounds[1][:, None])
    distance = jnp.abs(row_level - col_level).astype(f32)
    return jnp.where(inside, jnp.exp(-distance / vertical_scale), jnp.zeros_like(distance))


def edge_picker(width, depth):
    row = lax.broadcasted_iota(jnp.int32, (2 * depth, width), 0)
    col = lax.broadcasted_iota(jnp.int32, (2 * depth, width), 1)
    return jnp.where(col == jnp.where(row < depth, row, width - 2 * depth + row), 1.0, 0.0)


def params(grid_dims=0):
    if grid_dims:
        return pltpu.CompilerParams(
            dimension_semantics=("arbitrary",) * grid_dims, vmem_limit_bytes=56 << 20
        )
    return pltpu.CompilerParams(vmem_limit_bytes=56 << 20)


def write_edges(tile, rows_ref, cols_ref, rows, depth):
    width = tile(0).shape[1]
    for d in range(depth):
        rows_ref[0, 0, d] = tile(d).astype(bf16)
        rows_ref[1, 0, d] = tile(rows - depth + d).astype(bf16)
    picker = edge_picker(width, depth).astype(bf16)
    stack = jnp.concatenate([tile(y).astype(bf16) for y in range(rows)], axis=0)
    picked = lax.dot_general(picker, stack, NT, preferred_element_type=f32)
    cols_ref[0, 0] = picked[:depth].astype(bf16)
    cols_ref[1, 0] = picked[depth:].astype(bf16)


def kappa_parts(value, levels):
    high = value.astype(bf16).astype(f32)
    middle = (value - high).astype(bf16).astype(f32)
    low = value - high - middle
    level = lax.broadcasted_iota(jnp.int32, (levels, value.shape[1]), 0)
    return jnp.where(
        level == 0, high, jnp.where(level == 1, middle, jnp.where(level == 2, low, 0.0))
    )


def pack_kernel(rows, levels, depth, kappa_ref, field_ref, rows_ref, cols_ref):
    step = pl.program_id(0)
    last = pl.num_programs(0) - 1

    @pl.when(step < last)
    def _():
        write_edges(
            lambda y: field_ref[0, pl.ds(y, levels, stride=rows), :],
            rows_ref, cols_ref, rows, depth,
        )

    @pl.when(step == last)
    def _():
        write_edges(
            lambda y: kappa_parts(kappa_ref[y : y + 1, :], levels), rows_ref, cols_ref, rows, depth
        )


def edge_shapes(members, rows, levels, width, depth):
    shapes = [
        jax.ShapeDtypeStruct((2, members, depth, levels, width), bf16),
        jax.ShapeDtypeStruct((2, members, depth, rows * levels), bf16),
    ]
    specs = [
        pl.BlockSpec((2, 1, depth, levels, width), lambda k: (0, k, 0, 0, 0)),
        pl.BlockSpec((2, 1, depth, rows * levels), lambda k: (0, k, 0, 0)),
    ]
    return shapes, specs


def exchange_kernel(
    part, row_ref, col_ref, south, north, east, west, south_east, south_west, north_east,
    north_west, send, recv,
):
    gx, gy = lax.axis_index("gx"), lax.axis_index("gy")
    gx_count, gy_count = lax.axis_size("gx"), lax.axis_size("gy")
    to_east = {"gx": lax.rem(gx + 1, gx_count)}
    to_west = {"gx": lax.rem(gx + gx_count - 1, gx_count)}
    to_north = {"gy": gy - 1}
    to_south = {"gy": gy + 1}
    has_north = gy > 0
    has_south = gy < gy_count - 1
    barrier = pltpu.get_barrier_semaphore()

    def greet(device):
        pl.semaphore_signal(
            barrier, inc=1, device_id=device, device_id_type=pl.DeviceIdType.MESH
        )

    def copy(source, target, place, device):
        return pltpu.make_async_remote_copy(
            src_ref=source, dst_ref=target, send_sem=send.at[place], recv_sem=recv.at[place],
            device_id=device, device_id_type=pl.DeviceIdType.MESH,
        )

    cols = [copy(col_ref.at[0], east, 0, to_west), copy(col_ref.at[1], west, 1, to_east)]
    lanes = east.shape[2]
    first, final = pl.ds(0, part), pl.ds(lanes - part, part)
    up = [
        copy(row_ref.at[0], south, 2, to_north),
        copy(east.at[:, :, first], south_east, 4, to_north),
        copy(west.at[:, :, first], south_west, 5, to_north),
    ]
    down = [
        copy(row_ref.at[1], north, 3, to_south),
        copy(east.at[:, :, final], north_east, 6, to_south),
        copy(west.at[:, :, final], north_west, 7, to_south),
    ]
    greet(to_east)
    greet(to_west)
    pl.when(has_north)(lambda: greet(to_north))
    pl.when(has_south)(lambda: greet(to_south))
    peers = 2 + has_north.astype(jnp.int32) + has_south.astype(jnp.int32)
    pl.semaphore_wait(barrier, peers)
    for item in cols:
        item.start()
    pl.when(has_north)(lambda: up[0].start())
    pl.when(has_south)(lambda: down[0].start())

    @pl.when(jnp.logical_not(has_north))
    def _():
        for item in (north, north_east, north_west):
            item[...] = jnp.zeros_like(item)

    @pl.when(jnp.logical_not(has_south))
    def _():
        for item in (south, south_east, south_west):
            item[...] = jnp.zeros_like(item)

    for item in cols:
        item.wait_recv()

    @pl.when(has_north)
    def _():
        up[1].start()
        up[2].start()

    @pl.when(has_south)
    def _():
        down[1].start()
        down[2].start()

    for item in cols:
        item.wait_send()

    @pl.when(has_north)
    def _():
        for item in up:
            item.wait_send()
        for item in down:
            item.wait_recv()

    @pl.when(has_south)
    def _():
        for item in down:
            item.wait_send()
        for item in up:
            item.wait_recv()


def exchange(row_edges, col_edges, levels, depth, collective):
    members, lanes = col_edges.shape[1], col_edges.shape[3]
    part = depth * levels
    row = jax.ShapeDtypeStruct(row_edges.shape[1:], bf16)
    side = jax.ShapeDtypeStruct((members, depth, lanes), bf16)
    corner = jax.ShapeDtypeStruct((members, depth, part), bf16)
    vmem = pl.BlockSpec(memory_space=pltpu.VMEM)
    return pl.pallas_call(
        lambda *refs: exchange_kernel(part, *refs),
        in_specs=[vmem] * 2,
        out_specs=[vmem] * 8,
        out_shape=[row, row, side, side, corner, corner, corner, corner],
        scratch_shapes=[pltpu.SemaphoreType.DMA((8,)), pltpu.SemaphoreType.DMA((8,))],
        compiler_params=pltpu.CompilerParams(collective_id=collective, has_side_effects=True),
        name="exchange",
    )(row_edges, col_edges)


def halo_specs(members, rows, levels, width, depth, place):
    row = pl.BlockSpec((1, depth, levels, width), lambda k: (place(k), 0, 0, 0))
    side = pl.BlockSpec((1, depth, rows * levels), lambda k: (place(k), 0, 0))
    corner = pl.BlockSpec((1, depth, depth * levels), lambda k: (place(k), 0, 0))
    return [row, row, side, side, corner, corner, corner, corner]


def side_lanes(halo, width, depth):
    south, north, east, west, south_east, south_west, north_east, north_west = halo
    picker = edge_picker(width, depth).astype(bf16)
    easts = jnp.concatenate([east[0], south_east[0], north_east[0]], axis=1)
    wests = jnp.concatenate([west[0], south_west[0], north_west[0]], axis=1)
    return lax.dot_general(
        easts, picker[:depth], TN, preferred_element_type=f32
    ) + lax.dot_general(wests, picker[depth:], TN, preferred_element_type=f32)


def fill_ring(tile, halo, ring, rows, levels, width, depth):
    total = rows + 2 * depth
    for y in range(rows):
        ring[y, :, :width] = tile(y)
    for d in range(depth):
        ring[rows + d, :, :width] = halo[0][0, d].astype(f32)
        ring[rows + depth + d, :, :width] = halo[1][0, d].astype(f32)
    side = side_lanes(halo, width, depth)
    for y in range(total):
        ring[y, :, width:] = side[y * levels : (y + 1) * levels]


def fill_kappa(kappa_ref, halo, out_ref, rows, levels, width, depth):
    out_ref[:rows, :width] = kappa_ref[...]
    for d in range(depth):
        for base, ref in ((rows, halo[0]), (rows + depth, halo[1])):
            out_ref[base + d : base + d + 1, :width] = jnp.sum(
                ref[0, d].astype(f32), axis=0, keepdims=True
            )
    side = side_lanes(halo, width, depth)
    for y in range(rows + 2 * depth):
        out_ref[y : y + 1, width:] = jnp.sum(
            side[y * levels : (y + 1) * levels], axis=0, keepdims=True
        )


def diffuse(ring_a, ring_b, kappa_ref, edge_ref, rows, width, depth, adjoint):
    total = rows + 2 * depth
    at_top = edge_ref[0] == 1
    at_bottom = edge_ref[1] == 1
    source, target = ring_a, ring_b
    for step in range(1, depth + 1):
        wanted = list(range(rows + depth + step, total)) + list(range(rows + depth - step))
        keep = width if step == depth else 2 * width
        plain, loaded = {}, {}

        def load(y):
            if y not in loaded:
                plain[y] = source[y]
                loaded[y] = kappa_ref[pl.ds(y, 1), :] * plain[y] if adjoint else plain[y]
            return loaded[y]

        for y in wanted:
            north = load((y - 1) % total)
            center = load(y)
            south = load((y + 1) % total)
            if y == 0:
                north = jnp.where(at_top, center, north)
            if y == rows - 1:
                south = jnp.where(at_bottom, center, south)
            west = pltpu.roll(center, 1, 1)
            east = pltpu.roll(center, 2 * width - 1, 1)
            change = ((north + south) + (west + east)) - 4.0 * center
            if adjoint:
                result = plain[y] + change
            else:
                result = center + kappa_ref[pl.ds(y, 1), :] * change
            target[y, :, :keep] = result[:, :keep]
        source, target = target, source
    return source


def forward_kernel(dims, ens_scale, edge_ref, alpha_ref, kappa_ref, *refs):
    rows, levels, width, variables, depth = dims
    halo, refs = refs[:8], refs[8:]
    vertical_ref, perturb_ref, static_ref, out_ref, ring_ref, ring_a, ring_b, spread, acc = refs
    step = pl.program_id(0)
    count = rows * levels

    @pl.when(step == 0)
    def _():
        fill_kappa(kappa_ref, halo, ring_ref, rows, levels, width, depth)
        acc[...] = jnp.zeros_like(acc)

    @pl.when(step > 0)
    def _():
        fill_ring(
            lambda y: alpha_ref[0, pl.ds(y, levels, stride=rows), :],
            halo, ring_a, rows, levels, width, depth,
        )
        done = diffuse(ring_a, ring_b, ring_ref, edge_ref, rows, width, depth, False)
        for y in range(rows):
            spread[pl.ds(y, levels, stride=rows), :] = jnp.dot(
                vertical_ref[...], done[y, :, :width], precision=highest,
                preferred_element_type=f32,
            )
        for v in range(variables):
            acc[v * count : (v + 1) * count] += perturb_ref[0, v].astype(f32) * spread[...]

    @pl.when(step == pl.num_programs(0) - 1)
    def _():
        for y in range(rows):
            column = acc[pl.ds(y, variables * levels, stride=rows), :]
            out_ref[y] = ens_scale * column.T + static_ref[y]


def backward_kernel(
    dims, ens_scale, perturb_ref, grad_ref, main_ref, rows_ref, cols_ref, grad, field,
):
    rows, levels, width, variables, depth = dims

    @pl.when(pl.program_id(0) == 0)
    def _():
        for y in range(rows):
            grad[pl.ds(y, variables * levels, stride=rows), :] = ens_scale * grad_ref[y].T

    count = rows * levels
    total = perturb_ref[0, 0].astype(f32) * grad[:count]
    for v in range(1, variables):
        total = total + perturb_ref[0, v].astype(f32) * grad[v * count : (v + 1) * count]
    field[...] = total
    for y in range(rows):
        main_ref[0, y] = field[pl.ds(y, levels, stride=rows), :]
    write_edges(
        lambda y: field[pl.ds(y, levels, stride=rows), :], rows_ref, cols_ref, rows, depth
    )


def adjoint_kernel(dims, edge_ref, alpha_ref, main_ref, *refs):
    rows, levels, width, variables, depth = dims
    halo, refs = refs[:8], refs[8:]
    kappa_ref, vertical_ref, out_ref, ring_a, ring_b = refs
    fill_ring(lambda y: main_ref[0, y], halo, ring_a, rows, levels, width, depth)
    done = diffuse(ring_a, ring_b, kappa_ref, edge_ref, rows, width, depth, True)
    for y in range(rows):
        out_ref[0, pl.ds(y, levels, stride=rows), :] = alpha_ref[
            0, pl.ds(y, levels, stride=rows), :
        ] + jnp.dot(
            vertical_ref[...], done[y, :, :width], precision=highest, preferred_element_type=f32
        )


def split(value):
    high = value.astype(bf16)
    return high, (value - high.astype(f32)).astype(bf16)


def observe_kernel(
    rows, band, padded, count_ref, table_ref, anchor_ref, weight_ref, background_ref, observed_ref,
    inv_var_ref, jacobian_ref, out_ref, high_ref, low_ref,
):
    places = anchor_ref.shape[1]
    anchor = anchor_ref[...]
    anchor_row = anchor // band
    anchor_col = anchor - anchor_row * band
    slot = lax.broadcasted_iota(jnp.int32, (padded, places), 0)
    at_left = slot == anchor_col
    at_right = slot == anchor_col + 1
    total = background_ref[...].astype(f32).T
    for y in range(rows):
        upper = anchor_row == y
        lower = anchor_row == y - 1
        zero = jnp.zeros(anchor.shape, f32)
        left = jnp.where(upper, weight_ref[0:1], jnp.where(lower, weight_ref[2:3], zero))
        right = jnp.where(upper, weight_ref[1:2], jnp.where(lower, weight_ref[3:4], zero))
        weights = jnp.where(at_left, left, jnp.where(at_right, right, 0.0))
        high, low = split(weights)
        high_ref[y] = high
        low_ref[y] = low
        cells = table_ref[y]
        total = total + lax.dot_general(cells, high, TN, preferred_element_type=f32)
        total = total + lax.dot_general(cells, low, TN, preferred_element_type=f32)
    bent = jnp.tanh(total)
    modeled = jnp.dot(jacobian_ref[...], bent, precision=highest, preferred_element_type=f32)
    position = lax.broadcasted_iota(jnp.int32, modeled.shape, 1)
    misfit = jnp.where(
        position < count_ref[0], (modeled - observed_ref[...]) * inv_var_ref[...], 0.0
    )
    back = lax.dot_general(
        jacobian_ref[...], misfit, TN, precision=highest, preferred_element_type=f32
    )
    state_high, state_low = split((1.0 - bent * bent) * back)
    for y in range(rows):
        high = high_ref[y]
        cells = lax.dot_general(high, state_high, NT, preferred_element_type=f32)
        cells = cells + lax.dot_general(low_ref[y], state_high, NT, preferred_element_type=f32)
        cells = cells + lax.dot_general(high, state_low, NT, preferred_element_type=f32)
        out_ref[y] = cells


def choose(index, options):
    result = options[0]
    for place in range(1, len(options)):
        result = jnp.where(index == place, options[place], result)
    return result


def body(
    alpha, perturb, chi, kappa, vert_bounds, static_vert, fine_owner, obs_stencil, obs_weight,
    background, observed, inv_var, jacobian, obs_count,
):
    members, levels, rows, width = alpha.shape
    variables = perturb.shape[1]
    column = variables * levels
    depth = NDIFF
    groups = lax.axis_size("mem")
    band = width // groups
    shift = band // 2
    rim = shift + 1
    me = lax.axis_index("mem")
    count = rows * levels
    places = obs_stencil.shape[0]
    dims = (rows, levels, width, variables, depth)
    ens_scale = ensemble_weight / math.sqrt(members * groups - 1)
    gy_place = lax.axis_index("gy")
    edge = jnp.stack([gy_place == 0, gy_place == lax.axis_size("gy") - 1]).astype(jnp.int32)
    owners = fine_owner[0]
    band_ids = lax.iota(jnp.int32, groups)

    def band_of(group):
        return jnp.sum(jnp.where(owners == group, band_ids, 0))

    smem = pl.BlockSpec(memory_space=pltpu.SMEM)
    vmem = pl.BlockSpec(memory_space=pltpu.VMEM)
    member_block = pl.BlockSpec((1, count, width), lambda k: (k, 0, 0))
    perturb_block = pl.BlockSpec((1, variables, count, width), lambda k: (k, 0, 0, 0))
    ring_scratch = pltpu.VMEM((rows + 2 * depth, levels, 2 * width), f32)

    alpha_flat = alpha.reshape(members, count, width)
    perturb_flat = perturb.reshape(members, variables, count, width)
    vertical = vertical_matrix(vert_bounds, levels)

    edge_out, edge_specs = edge_shapes(members + 1, rows, levels, width, depth)
    row_edges, col_edges = pl.pallas_call(
        lambda *refs: pack_kernel(rows, levels, depth, *refs),
        grid=(members + 1,),
        in_specs=[
            vmem,
            pl.BlockSpec((1, count, width), lambda k: (jnp.minimum(k, members - 1), 0, 0)),
        ],
        out_specs=edge_specs,
        out_shape=edge_out,
        compiler_params=params(1),
        name="pack",
    )(kappa, alpha_flat)
    halo = exchange(row_edges, col_edges, levels, depth, 0)

    static = jnp.einsum("vlm,vmyx->yxvl", static_vert, chi, precision=highest)
    static = jnp.where(me == 0, static_weight * static, 0.0).reshape(rows, width, column)
    partial, kappa_all = pl.pallas_call(
        lambda *refs: forward_kernel(dims, ens_scale, *refs),
        grid=(members + 1,),
        in_specs=[
            smem,
            pl.BlockSpec((1, count, width), lambda k: (jnp.maximum(k - 1, 0), 0, 0)),
            vmem,
            *halo_specs(
                members + 1, rows, levels, width, depth,
                lambda k: jnp.where(k == 0, members, k - 1),
            ),
            vmem,
            pl.BlockSpec(
                (1, variables, count, width), lambda k: (jnp.maximum(k - 1, 0), 0, 0, 0)
            ),
            vmem,
        ],
        out_specs=[
            pl.BlockSpec((rows, width, column), lambda k: (0, 0, 0)),
            pl.BlockSpec((rows + 2 * depth, 2 * width), lambda k: (0, 0)),
        ],
        out_shape=[
            jax.ShapeDtypeStruct((rows, width, column), f32),
            jax.ShapeDtypeStruct((rows + 2 * depth, 2 * width), f32),
        ],
        scratch_shapes=[
            ring_scratch,
            ring_scratch,
            pltpu.VMEM((count, width), f32),
            pltpu.VMEM((variables * count, width), f32),
        ],
        compiler_params=params(1),
        name="forward",
    )(edge, alpha_flat, kappa, *halo, vertical, perturb_flat, static)

    east_rim = shifted(partial[:, :rim].astype(bf16), "gx", -1)
    wide = jnp.concatenate([partial, east_rim.astype(f32)], axis=1)
    regions = [wide[:, b * band + shift : b * band + shift + band + 1] for b in range(groups)]
    own_band = band_of(me)
    increment = choose(own_band, regions)
    for hop in range(1, groups):
        away = choose(band_of((me + hop) % groups), regions).astype(bf16)
        increment = increment + shifted(away, "mem", hop).astype(f32)
    padded = -(-(band + 1) // 16) * 16
    table = jnp.pad(increment.astype(bf16), ((0, 0), (0, padded - band - 1), (0, 0)))

    region_grad = pl.pallas_call(
        lambda *refs: observe_kernel(rows, band, padded, *refs),
        in_specs=[smem] + [vmem] * 7,
        out_specs=vmem,
        out_shape=jax.ShapeDtypeStruct((rows, padded, column), f32),
        scratch_shapes=[
            pltpu.VMEM((rows, padded, places), bf16),
            pltpu.VMEM((rows, padded, places), bf16),
        ],
        compiler_params=params(),
        name="observe",
    )(
        obs_count, table, obs_stencil.reshape(1, places), obs_weight, background, observed,
        inv_var, jacobian,
    )

    region_grad = region_grad[:, : band + 1]
    pieces = [(own_band, region_grad)]
    for hop in range(1, groups):
        pieces.append((band_of((me - hop) % groups), shifted(region_grad, "mem", hop)))
    wide_grad = jnp.zeros((rows, width + rim, column), f32)
    for b in range(groups):
        placed = choose_equal(b, pieces)
        before = b * band + shift
        after = width + rim - before - band - 1
        wide_grad = wide_grad + jnp.pad(placed, ((0, 0), (before, after), (0, 0)))
    west_rim = shifted(wide_grad[:, width:], "gx", 1)
    grad_cells = wide_grad[:, :width] + jnp.pad(west_rim, ((0, 0), (0, width - rim), (0, 0)))

    edge_out, edge_specs = edge_shapes(members, rows, levels, width, depth)
    main, row_edges, col_edges = pl.pallas_call(
        lambda *refs: backward_kernel(dims, ens_scale, *refs),
        grid=(members,),
        in_specs=[perturb_block, vmem],
        out_specs=[pl.BlockSpec((1, rows, levels, width), lambda k: (k, 0, 0, 0))] + edge_specs,
        out_shape=[jax.ShapeDtypeStruct((members, rows, levels, width), f32)] + edge_out,
        scratch_shapes=[
            pltpu.VMEM((variables * count, width), f32),
            pltpu.VMEM((count, width), f32),
        ],
        compiler_params=params(1),
        name="backward",
    )(perturb_flat, grad_cells)
    halo = exchange(row_edges, col_edges, levels, depth, 1)
    grad_chi = chi + static_weight * jnp.einsum(
        "vlm,yxvl->vmyx",
        static_vert,
        grad_cells.reshape(rows, width, variables, levels),
        precision=highest,
    )
    grad_alpha = pl.pallas_call(
        lambda *refs: adjoint_kernel(dims, *refs),
        grid=(members,),
        in_specs=[
            smem, member_block, pl.BlockSpec((1, rows, levels, width), lambda k: (k, 0, 0, 0)),
            *halo_specs(members, rows, levels, width, depth, lambda k: k), vmem, vmem,
        ],
        out_specs=member_block,
        out_shape=jax.ShapeDtypeStruct((members, count, width), f32),
        scratch_shapes=[ring_scratch, ring_scratch],
        compiler_params=params(1),
        name="adjoint",
    )(edge, alpha_flat, main, *halo, kappa_all, vertical.T)
    return (grad_alpha.reshape(alpha.shape), grad_chi)


def choose_equal(wanted, pieces):
    result = pieces[0][1]
    for index, piece in pieces[1:]:
        result = jnp.where(index == wanted, piece, result)
    return result


def solution(mesh):
    in_specs = (
        P("mem", None, "gy", "gx"),
        P("mem", None, None, "gy", "gx"),
        P(None, None, "gy", "gx"),
        P("gy", "gx"),
        P(),
        P(),
        P(("gy", "gx"), None),
        P(("mem", "gy", "gx")),
        P(None, ("mem", "gy", "gx")),
        P(("mem", "gy", "gx"), None),
        P(None, ("mem", "gy", "gx")),
        P(None, ("mem", "gy", "gx")),
        P(),
        P(("mem", "gy", "gx")),
    )
    out_specs = (P("mem", None, "gy", "gx"), P(None, None, "gy", "gx"))
    return jax.shard_map(body, mesh=mesh, in_specs=in_specs, out_specs=out_specs, check_vma=False)
```

```python
import math

import jax
import jax.numpy as jnp
from jax import lax
from jax.experimental import pallas as pl
from jax.experimental.pallas import tpu as pltpu
from jax.sharding import PartitionSpec as P

NDIFF = 4

ensemble_weight = 0.8
static_weight = 0.6
vertical_scale = 2.0
highest = lax.Precision.HIGHEST
f32 = jnp.float32
bf16 = jnp.bfloat16
NT = (((1,), (1,)), ((), ()))
TN = (((0,), (0,)), ((), ()))


def shifted(value, axis, steps):
    count = lax.axis_size(axis)
    pairs = [(source, (source + steps) % count) for source in range(count)]
    return lax.ppermute(value, axis, pairs)


def vertical_matrix(vert_bounds, levels):
    row_level = lax.broadcasted_iota(jnp.int32, (levels, levels), 0)
    col_level = lax.broadcasted_iota(jnp.int32, (levels, levels), 1)
    inside = (col_level >= vert_bounds[0][:, None]) & (col_level <= vert_bounds[1][:, None])
    distance = jnp.abs(row_level - col_level).astype(f32)
    return jnp.where(inside, jnp.exp(-distance / vertical_scale), jnp.zeros_like(distance))


def edge_picker(width, depth):
    row = lax.broadcasted_iota(jnp.int32, (2 * depth, width), 0)
    col = lax.broadcasted_iota(jnp.int32, (2 * depth, width), 1)
    return jnp.where(col == jnp.where(row < depth, row, width - 2 * depth + row), 1.0, 0.0)


def params(grid_dims=0):
    if grid_dims:
        return pltpu.CompilerParams(
            dimension_semantics=("arbitrary",) * grid_dims, vmem_limit_bytes=56 << 20
        )
    return pltpu.CompilerParams(vmem_limit_bytes=56 << 20)


def write_edges(tile, rows_ref, cols_ref, rows, depth):
    width = tile(0).shape[1]
    for d in range(depth):
        rows_ref[0, 0, d] = tile(d).astype(bf16)
        rows_ref[1, 0, d] = tile(rows - depth + d).astype(bf16)
    picker = edge_picker(width, depth).astype(bf16)
    stack = jnp.concatenate([tile(y).astype(bf16) for y in range(rows)], axis=0)
    picked = lax.dot_general(picker, stack, NT, preferred_element_type=f32)
    cols_ref[0, 0] = picked[:depth].astype(bf16)
    cols_ref[1, 0] = picked[depth:].astype(bf16)


def kappa_parts(value, levels):
    high = value.astype(bf16).astype(f32)
    middle = (value - high).astype(bf16).astype(f32)
    low = value - high - middle
    level = lax.broadcasted_iota(jnp.int32, (levels, value.shape[1]), 0)
    return jnp.where(
        level == 0, high, jnp.where(level == 1, middle, jnp.where(level == 2, low, 0.0))
    )


def pack_kernel(rows, levels, depth, kappa_ref, field_ref, rows_ref, cols_ref):
    step = pl.program_id(0)
    last = pl.num_programs(0) - 1

    @pl.when(step < last)
    def _():
        write_edges(
            lambda y: field_ref[0, pl.ds(y, levels, stride=rows), :],
            rows_ref, cols_ref, rows, depth,
        )

    @pl.when(step == last)
    def _():
        write_edges(
            lambda y: kappa_parts(kappa_ref[y : y + 1, :], levels), rows_ref, cols_ref, rows, depth
        )


def edge_shapes(members, rows, levels, width, depth):
    shapes = [
        jax.ShapeDtypeStruct((2, members, depth, levels, width), bf16),
        jax.ShapeDtypeStruct((2, members, depth, rows * levels), bf16),
    ]
    specs = [
        pl.BlockSpec((2, 1, depth, levels, width), lambda k: (0, k, 0, 0, 0)),
        pl.BlockSpec((2, 1, depth, rows * levels), lambda k: (0, k, 0, 0)),
    ]
    return shapes, specs


def exchange_kernel(
    part, row_ref, col_ref, south, north, east, west, south_east, south_west, north_east,
    north_west, send, recv,
):
    gx, gy = lax.axis_index("gx"), lax.axis_index("gy")
    gx_count, gy_count = lax.axis_size("gx"), lax.axis_size("gy")
    to_east = {"gx": lax.rem(gx + 1, gx_count)}
    to_west = {"gx": lax.rem(gx + gx_count - 1, gx_count)}
    to_north = {"gy": gy - 1}
    to_south = {"gy": gy + 1}
    has_north = gy > 0
    has_south = gy < gy_count - 1
    barrier = pltpu.get_barrier_semaphore()

    def greet(device):
        pl.semaphore_signal(
            barrier, inc=1, device_id=device, device_id_type=pl.DeviceIdType.MESH
        )

    def copy(source, target, place, device):
        return pltpu.make_async_remote_copy(
            src_ref=source, dst_ref=target, send_sem=send.at[place], recv_sem=recv.at[place],
            device_id=device, device_id_type=pl.DeviceIdType.MESH,
        )

    cols = [copy(col_ref.at[0], east, 0, to_west), copy(col_ref.at[1], west, 1, to_east)]
    lanes = east.shape[2]
    first, final = pl.ds(0, part), pl.ds(lanes - part, part)
    up = [
        copy(row_ref.at[0], south, 2, to_north),
        copy(east.at[:, :, first], south_east, 4, to_north),
        copy(west.at[:, :, first], south_west, 5, to_north),
    ]
    down = [
        copy(row_ref.at[1], north, 3, to_south),
        copy(east.at[:, :, final], north_east, 6, to_south),
        copy(west.at[:, :, final], north_west, 7, to_south),
    ]
    greet(to_east)
    greet(to_west)
    pl.when(has_north)(lambda: greet(to_north))
    pl.when(has_south)(lambda: greet(to_south))
    peers = 2 + has_north.astype(jnp.int32) + has_south.astype(jnp.int32)
    pl.semaphore_wait(barrier, peers)
    for item in cols:
        item.start()
    pl.when(has_north)(lambda: up[0].start())
    pl.when(has_south)(lambda: down[0].start())

    @pl.when(jnp.logical_not(has_north))
    def _():
        for item in (north, north_east, north_west):
            item[...] = jnp.zeros_like(item)

    @pl.when(jnp.logical_not(has_south))
    def _():
        for item in (south, south_east, south_west):
            item[...] = jnp.zeros_like(item)

    for item in cols:
        item.wait_recv()

    @pl.when(has_north)
    def _():
        up[1].start()
        up[2].start()

    @pl.when(has_south)
    def _():
        down[1].start()
        down[2].start()

    for item in cols:
        item.wait_send()

    @pl.when(has_north)
    def _():
        for item in up:
            item.wait_send()
        for item in down:
            item.wait_recv()

    @pl.when(has_south)
    def _():
        for item in down:
            item.wait_send()
        for item in up:
            item.wait_recv()


def exchange(row_edges, col_edges, levels, depth, collective):
    members, lanes = col_edges.shape[1], col_edges.shape[3]
    part = depth * levels
    row = jax.ShapeDtypeStruct(row_edges.shape[1:], bf16)
    side = jax.ShapeDtypeStruct((members, depth, lanes), bf16)
    corner = jax.ShapeDtypeStruct((members, depth, part), bf16)
    vmem = pl.BlockSpec(memory_space=pltpu.VMEM)
    return pl.pallas_call(
        lambda *refs: exchange_kernel(part, *refs),
        in_specs=[vmem] * 2,
        out_specs=[vmem] * 8,
        out_shape=[row, row, side, side, corner, corner, corner, corner],
        scratch_shapes=[pltpu.SemaphoreType.DMA((8,)), pltpu.SemaphoreType.DMA((8,))],
        compiler_params=pltpu.CompilerParams(collective_id=collective, has_side_effects=True),
        name="exchange",
    )(row_edges, col_edges)


def side_lanes(halo, member, width, depth):
    south, north, east, west, south_east, south_west, north_east, north_west = halo
    picker = edge_picker(width, depth).astype(bf16)
    easts = jnp.concatenate([east[member], south_east[member], north_east[member]], axis=1)
    wests = jnp.concatenate([west[member], south_west[member], north_west[member]], axis=1)
    return lax.dot_general(
        easts, picker[:depth], TN, preferred_element_type=f32
    ) + lax.dot_general(wests, picker[depth:], TN, preferred_element_type=f32)


def fill_ring(tile, halo, member, ring, rows, levels, width, depth):
    total = rows + 2 * depth
    for y in range(rows):
        ring[y, :, :width] = tile(y)
    for d in range(depth):
        ring[rows + d, :, :width] = halo[0][member, d].astype(f32)
        ring[rows + depth + d, :, :width] = halo[1][member, d].astype(f32)
    side = side_lanes(halo, member, width, depth)
    for y in range(total):
        ring[y, :, width:] = side[y * levels : (y + 1) * levels]


def fill_kappa(kappa_ref, halo, member, out_ref, rows, levels, width, depth):
    out_ref[:rows, :width] = kappa_ref[...]
    for d in range(depth):
        for base, ref in ((rows, halo[0]), (rows + depth, halo[1])):
            out_ref[base + d : base + d + 1, :width] = jnp.sum(
                ref[member, d].astype(f32), axis=0, keepdims=True
            )
    side = side_lanes(halo, member, width, depth)
    for y in range(rows + 2 * depth):
        out_ref[y : y + 1, width:] = jnp.sum(
            side[y * levels : (y + 1) * levels], axis=0, keepdims=True
        )


def diffuse(ring_a, ring_b, kappa_ref, rows, width, depth, adjoint):
    total = rows + 2 * depth
    at_top = lax.axis_index("gy") == 0
    at_bottom = lax.axis_index("gy") == lax.axis_size("gy") - 1
    source, target = ring_a, ring_b
    for step in range(1, depth + 1):
        wanted = list(range(rows + depth + step, total)) + list(range(rows + depth - step))
        keep = width if step == depth else 2 * width
        plain, loaded = {}, {}

        def load(y):
            if y not in loaded:
                plain[y] = source[y]
                loaded[y] = kappa_ref[pl.ds(y, 1), :] * plain[y] if adjoint else plain[y]
            return loaded[y]

        for y in wanted:
            north = load((y - 1) % total)
            center = load(y)
            south = load((y + 1) % total)
            if y == 0:
                north = jnp.where(at_top, center, north)
            if y == rows - 1:
                south = jnp.where(at_bottom, center, south)
            west = pltpu.roll(center, 1, 1)
            east = pltpu.roll(center, 2 * width - 1, 1)
            change = ((north + south) + (west + east)) - 4.0 * center
            if adjoint:
                result = plain[y] + change
            else:
                result = center + kappa_ref[pl.ds(y, 1), :] * change
            target[y, :, :keep] = result[:, :keep]
        source, target = target, source
    return source


def forward_kernel(dims, ens_scale, alpha_ref, kappa_ref, *refs):
    rows, levels, width, variables, depth = dims
    halo, refs = refs[:8], refs[8:]
    vertical_ref, perturb_ref, static_ref, out_ref, ring_ref, ring_a, ring_b, spread, acc = refs
    step = pl.program_id(0)
    count = rows * levels

    @pl.when(step == 0)
    def _():
        fill_kappa(kappa_ref, halo, halo[0].shape[0] - 1, ring_ref, rows, levels, width, depth)
        acc[...] = jnp.zeros_like(acc)

    @pl.when(step > 0)
    def _():
        fill_ring(
            lambda y: alpha_ref[0, pl.ds(y, levels, stride=rows), :],
            halo, step - 1, ring_a, rows, levels, width, depth,
        )
        done = diffuse(ring_a, ring_b, ring_ref, rows, width, depth, False)
        for y in range(rows):
            spread[pl.ds(y, levels, stride=rows), :] = jnp.dot(
                vertical_ref[...], done[y, :, :width], precision=highest,
                preferred_element_type=f32,
            )
        for v in range(variables):
            acc[v * count : (v + 1) * count] += perturb_ref[0, v].astype(f32) * spread[...]

    @pl.when(step == pl.num_programs(0) - 1)
    def _():
        for y in range(rows):
            column = acc[pl.ds(y, variables * levels, stride=rows), :]
            out_ref[y] = ens_scale * column.T + static_ref[y]


def backward_kernel(
    dims, ens_scale, perturb_ref, grad_ref, main_ref, rows_ref, cols_ref, grad, field,
):
    rows, levels, width, variables, depth = dims

    @pl.when(pl.program_id(0) == 0)
    def _():
        for y in range(rows):
            grad[pl.ds(y, variables * levels, stride=rows), :] = ens_scale * grad_ref[y].T

    count = rows * levels
    total = perturb_ref[0, 0].astype(f32) * grad[:count]
    for v in range(1, variables):
        total = total + perturb_ref[0, v].astype(f32) * grad[v * count : (v + 1) * count]
    field[...] = total
    for y in range(rows):
        main_ref[0, y] = field[pl.ds(y, levels, stride=rows), :]
    write_edges(
        lambda y: field[pl.ds(y, levels, stride=rows), :], rows_ref, cols_ref, rows, depth
    )


def adjoint_kernel(dims, alpha_ref, main_ref, *refs):
    rows, levels, width, variables, depth = dims
    halo, refs = refs[:8], refs[8:]
    kappa_ref, vertical_ref, out_ref, ring_a, ring_b = refs
    fill_ring(lambda y: main_ref[0, y], halo, pl.program_id(0), ring_a, rows, levels, width, depth)
    done = diffuse(ring_a, ring_b, kappa_ref, rows, width, depth, True)
    for y in range(rows):
        out_ref[0, pl.ds(y, levels, stride=rows), :] = alpha_ref[
            0, pl.ds(y, levels, stride=rows), :
        ] + jnp.dot(
            vertical_ref[...], done[y, :, :width], precision=highest, preferred_element_type=f32
        )


def split(value):
    high = value.astype(bf16)
    return high, (value - high.astype(f32)).astype(bf16)


def observe_kernel(
    rows, band, padded, count_ref, table_ref, anchor_ref, weight_ref, background_ref, observed_ref,
    inv_var_ref, jacobian_ref, out_ref, high_ref, low_ref,
):
    places = anchor_ref.shape[1]
    anchor = anchor_ref[...]
    anchor_row = anchor // band
    anchor_col = anchor - anchor_row * band
    slot = lax.broadcasted_iota(jnp.int32, (padded, places), 0)
    at_left = slot == anchor_col
    at_right = slot == anchor_col + 1
    total = background_ref[...].astype(f32).T
    for y in range(rows):
        upper = anchor_row == y
        lower = anchor_row == y - 1
        zero = jnp.zeros(anchor.shape, f32)
        left = jnp.where(upper, weight_ref[0:1], jnp.where(lower, weight_ref[2:3], zero))
        right = jnp.where(upper, weight_ref[1:2], jnp.where(lower, weight_ref[3:4], zero))
        weights = jnp.where(at_left, left, jnp.where(at_right, right, 0.0))
        high, low = split(weights)
        high_ref[y] = high
        low_ref[y] = low
        cells = table_ref[y]
        total = total + lax.dot_general(cells, high, TN, preferred_element_type=f32)
        total = total + lax.dot_general(cells, low, TN, preferred_element_type=f32)
    bent = jnp.tanh(total)
    modeled = jnp.dot(jacobian_ref[...], bent, precision=highest, preferred_element_type=f32)
    position = lax.broadcasted_iota(jnp.int32, modeled.shape, 1)
    misfit = jnp.where(
        position < count_ref[0], (modeled - observed_ref[...]) * inv_var_ref[...], 0.0
    )
    back = lax.dot_general(
        jacobian_ref[...], misfit, TN, precision=highest, preferred_element_type=f32
    )
    state_high, state_low = split((1.0 - bent * bent) * back)
    for y in range(rows):
        high = high_ref[y]
        cells = lax.dot_general(high, state_high, NT, preferred_element_type=f32)
        cells = cells + lax.dot_general(low_ref[y], state_high, NT, preferred_element_type=f32)
        cells = cells + lax.dot_general(high, state_low, NT, preferred_element_type=f32)
        out_ref[y] = cells


def choose(index, options):
    result = options[0]
    for place in range(1, len(options)):
        result = jnp.where(index == place, options[place], result)
    return result


def body(
    alpha, perturb, chi, kappa, vert_bounds, static_vert, fine_owner, obs_stencil, obs_weight,
    background, observed, inv_var, jacobian, obs_count,
):
    members, levels, rows, width = alpha.shape
    variables = perturb.shape[1]
    column = variables * levels
    depth = NDIFF
    groups = lax.axis_size("mem")
    band = width // groups
    shift = band // 2
    rim = shift + 1
    me = lax.axis_index("mem")
    count = rows * levels
    places = obs_stencil.shape[0]
    dims = (rows, levels, width, variables, depth)
    ens_scale = ensemble_weight / math.sqrt(members * groups - 1)
    owners = fine_owner[0]
    band_ids = lax.iota(jnp.int32, groups)

    def band_of(group):
        return jnp.sum(jnp.where(owners == group, band_ids, 0))

    smem = pl.BlockSpec(memory_space=pltpu.SMEM)
    vmem = pl.BlockSpec(memory_space=pltpu.VMEM)
    member_block = pl.BlockSpec((1, count, width), lambda k: (k, 0, 0))
    perturb_block = pl.BlockSpec((1, variables, count, width), lambda k: (k, 0, 0, 0))
    ring_scratch = pltpu.VMEM((rows + 2 * depth, levels, 2 * width), f32)

    alpha_flat = alpha.reshape(members, count, width)
    perturb_flat = perturb.reshape(members, variables, count, width)
    vertical = vertical_matrix(vert_bounds, levels)

    edge_out, edge_specs = edge_shapes(members + 1, rows, levels, width, depth)
    row_edges, col_edges = pl.pallas_call(
        lambda *refs: pack_kernel(rows, levels, depth, *refs),
        grid=(members + 1,),
        in_specs=[
            vmem,
            pl.BlockSpec((1, count, width), lambda k: (jnp.minimum(k, members - 1), 0, 0)),
        ],
        out_specs=edge_specs,
        out_shape=edge_out,
        compiler_params=params(1),
        name="pack",
    )(kappa, alpha_flat)
    halo = exchange(row_edges, col_edges, levels, depth, 0)

    static = jnp.einsum("vlm,vmyx->yxvl", static_vert, chi, precision=highest)
    static = jnp.where(me == 0, static_weight * static, 0.0).reshape(rows, width, column)
    partial, kappa_all = pl.pallas_call(
        lambda *refs: forward_kernel(dims, ens_scale, *refs),
        grid=(members + 1,),
        in_specs=[
            pl.BlockSpec((1, count, width), lambda k: (jnp.maximum(k - 1, 0), 0, 0)),
            vmem,
            *[vmem] * 8,
            vmem,
            pl.BlockSpec(
                (1, variables, count, width), lambda k: (jnp.maximum(k - 1, 0), 0, 0, 0)
            ),
            vmem,
        ],
        out_specs=[
            pl.BlockSpec((rows, width, column), lambda k: (0, 0, 0)),
            pl.BlockSpec((rows + 2 * depth, 2 * width), lambda k: (0, 0)),
        ],
        out_shape=[
            jax.ShapeDtypeStruct((rows, width, column), f32),
            jax.ShapeDtypeStruct((rows + 2 * depth, 2 * width), f32),
        ],
        scratch_shapes=[
            ring_scratch,
            ring_scratch,
            pltpu.VMEM((count, width), f32),
            pltpu.VMEM((variables * count, width), f32),
        ],
        compiler_params=params(1),
        name="forward",
    )(alpha_flat, kappa, *halo, vertical, perturb_flat, static)

    own_band = band_of(me)
    east_rim = shifted(partial[:, :rim].astype(bf16), "gx", -1)
    near = [partial[:, b * band + shift : (b + 1) * band] for b in range(groups)]
    far = [partial[:, b * band : b * band + rim] for b in range(1, groups)]
    far.append(east_rim.astype(f32))
    halves = []
    for parts in (near, far):
        half = choose(own_band, parts)
        for hop in range(1, groups):
            away = choose(band_of((me + hop) % groups), parts).astype(bf16)
            half = half + shifted(away, "mem", hop).astype(f32)
        halves.append(half)
    increment = jnp.concatenate(halves, axis=1)
    padded = -(-(band + 1) // 16) * 16
    table = jnp.pad(increment.astype(bf16), ((0, 0), (0, padded - band - 1), (0, 0)))

    region_grad = pl.pallas_call(
        lambda *refs: observe_kernel(rows, band, padded, *refs),
        in_specs=[smem] + [vmem] * 7,
        out_specs=vmem,
        out_shape=jax.ShapeDtypeStruct((rows, padded, column), f32),
        scratch_shapes=[
            pltpu.VMEM((rows, padded, places), bf16),
            pltpu.VMEM((rows, padded, places), bf16),
        ],
        compiler_params=params(),
        name="observe",
    )(
        obs_count, table, obs_stencil.reshape(1, places), obs_weight, background, observed,
        inv_var, jacobian,
    )

    near, far = region_grad[:, : band - shift], region_grad[:, band - shift : band + 1]
    far_pieces = [(own_band, far)]
    for hop in range(1, groups):
        far_pieces.append((band_of((me - hop) % groups), shifted(far, "mem", hop)))
    rim_grad = choose_equal(groups - 1, far_pieces)
    near, rim_grad = lax.optimization_barrier((near, rim_grad))
    west_rim = shifted(rim_grad, "gx", 1)
    near_pieces = [(own_band, near)]
    for hop in range(1, groups):
        near_pieces.append((band_of((me - hop) % groups), shifted(near, "mem", hop)))
    grad_cells = jnp.pad(west_rim, ((0, 0), (0, width - rim), (0, 0)))
    for b in range(groups):
        before = b * band + shift
        grad_cells = grad_cells + jnp.pad(
            choose_equal(b, near_pieces), ((0, 0), (before, width - (b + 1) * band), (0, 0))
        )
    for b in range(1, groups):
        before = b * band
        grad_cells = grad_cells + jnp.pad(
            choose_equal(b - 1, far_pieces), ((0, 0), (before, width - before - rim), (0, 0))
        )

    edge_out, edge_specs = edge_shapes(members, rows, levels, width, depth)
    main, row_edges, col_edges = pl.pallas_call(
        lambda *refs: backward_kernel(dims, ens_scale, *refs),
        grid=(members,),
        in_specs=[perturb_block, vmem],
        out_specs=[pl.BlockSpec((1, rows, levels, width), lambda k: (k, 0, 0, 0))] + edge_specs,
        out_shape=[jax.ShapeDtypeStruct((members, rows, levels, width), f32)] + edge_out,
        scratch_shapes=[
            pltpu.VMEM((variables * count, width), f32),
            pltpu.VMEM((count, width), f32),
        ],
        compiler_params=params(1),
        name="backward",
    )(perturb_flat, grad_cells)
    halo = exchange(row_edges, col_edges, levels, depth, 1)
    grad_chi = chi + static_weight * jnp.einsum(
        "vlm,yxvl->vmyx",
        static_vert,
        grad_cells.reshape(rows, width, variables, levels),
        precision=highest,
    )
    grad_alpha = pl.pallas_call(
        lambda *refs: adjoint_kernel(dims, *refs),
        grid=(members,),
        in_specs=[
            member_block, pl.BlockSpec((1, rows, levels, width), lambda k: (k, 0, 0, 0)),
            *[vmem] * 8, vmem, vmem,
        ],
        out_specs=member_block,
        out_shape=jax.ShapeDtypeStruct((members, count, width), f32),
        scratch_shapes=[ring_scratch, ring_scratch],
        compiler_params=params(1),
        name="adjoint",
    )(alpha_flat, main, *halo, kappa_all, vertical.T)
    return (grad_alpha.reshape(alpha.shape), grad_chi)


def choose_equal(wanted, pieces):
    result = pieces[0][1]
    for index, piece in pieces[1:]:
        result = jnp.where(index == wanted, piece, result)
    return result


def solution(mesh):
    in_specs = (
        P("mem", None, "gy", "gx"),
        P("mem", None, None, "gy", "gx"),
        P(None, None, "gy", "gx"),
        P("gy", "gx"),
        P(),
        P(),
        P(("gy", "gx"), None),
        P(("mem", "gy", "gx")),
        P(None, ("mem", "gy", "gx")),
        P(("mem", "gy", "gx"), None),
        P(None, ("mem", "gy", "gx")),
        P(None, ("mem", "gy", "gx")),
        P(),
        P(("mem", "gy", "gx")),
    )
    out_specs = (P("mem", None, "gy", "gx"), P(None, None, "gy", "gx"))
    return jax.shard_map(body, mesh=mesh, in_specs=in_specs, out_specs=out_specs, check_vma=False)
```
